32 devices in a mesh: beam: 2 (over x), rng: 16 (over z, y, core).
Axes of the slice: x: 2, y: 2, z: 4, core: 2. Of those that a mesh axis runs over, the one named last changes fastest.
Arguments:
- echoes: bfloat16 [4, 1024, 8192], P('beam', 'rng'), parts along dimension 0, may hold values from -6 to 6
- phase_code: int32 [256], replicated, may hold values from -1 to 1, as said below
Outputs:
- test_ratio: float32 [2048, 8192], P('beam', 'rng'), parts along dimension 0
The draws below stay inside these ranges and needn't reach their ends.
There are 2 independent parts, one for each index of `beam`. The reference program is written for one: setup_inputs(seed, part) draws one part's arguments, and reference() takes and returns one part's arrays. A program takes and returns all parts, laid end to end along the dimension named above; an argument that names none is the same for every part. Nothing has to cross between parts.
Inputs may be any that keep to these rules, and one draw needn't show every extreme that they name: `phase_code`: each entry is -1 or +1.
All inputs are finite; a program needn't handle non-finite values.
Results may differ from the reference program's by a relative error of at most 0.0039.
Values may be sent and summed in bfloat16 or wider, within the bound.
A program may use at most 128 MiB of HBM per device.

```python
import math
import jax
import jax.numpy as jnp

PULSES = 1024
TAPS = 256
WIN_R = 33
WIN_D = 9
GUARD_R = 5
GUARD_D = 3
RANGE = 8192


def draw_phase_code(key, part):
    return (2 * jax.random.randint(key, (TAPS,), 0, 2) - 1).astype(jnp.int32)


def block_scale(own_key, dims, shards, smallest, largest):
    factor_of, own = 1.0, jax.random.fold_in(own_key, 6)
    for dim, blocks in shards:
        heights = jnp.exp(jax.random.uniform(jax.random.fold_in(own, dim), (blocks,), jnp.float32, smallest / len(shards), largest / len(shards)))
        factor_of = factor_of * jnp.repeat(heights, dims[dim] // blocks).reshape([-1 if axis == dim else 1 for axis in range(len(dims))])
    return factor_of


def noise(rng, dims, spread, most, shards=(), kind=jnp.bfloat16):
    drawn = jax.random.normal(rng, dims, jnp.float32) * spread
    if len(shards) > 0:
        drawn = block_scale(rng, dims, shards, -0.22, 0.18) * drawn
    return jnp.clip(drawn, min=-most, max=most).astype(kind)


def setup_inputs(seed: int = 0, part: int = 0) -> dict:
    key_list = jax.random.split(jax.random.key(seed), 3)
    part_keys = jax.random.split(jax.random.fold_in(key_list[2], part), 3)
    return {
        "echoes": noise(part_keys[0], (2, PULSES, RANGE), 1.0, 6.0, ((1, 16),)),
        "phase_code": draw_phase_code(jax.random.fold_in(key_list[2], 71), part),
    }


def toeplitz_pair(phase_code):
    length = phase_code.shape[0]
    row_index = jnp.arange(length, dtype=jnp.int32)[:, None]
    col_index = jnp.arange(length, dtype=jnp.int32)[None, :]
    values = phase_code.astype(jnp.float32)
    lag_here = row_index - col_index
    lag_next = row_index + length - col_index
    upper_part = jnp.where(lag_here >= 0, jnp.take(values, jnp.clip(lag_here, 0, length - 1)), 0.0)
    lower_part = jnp.where(lag_next < length, jnp.take(values, jnp.clip(lag_next, 0, length - 1)), 0.0)
    return jnp.concatenate([upper_part, lower_part], axis=0).astype(jnp.bfloat16)


def compress_rows(echo_rows, next_tail, filter_pair):
    length = filter_pair.shape[1]
    row_count = echo_rows.shape[0]
    cell_count = echo_rows.shape[1]
    blocks = cell_count // length
    upper_half = filter_pair[:length]
    lower_half = filter_pair[length:]
    block_rows = echo_rows.reshape(row_count * blocks, length)
    own_terms = jnp.dot(block_rows, upper_half, preferred_element_type=jnp.float32).reshape(row_count, blocks, length)
    next_terms = jnp.dot(block_rows, lower_half, preferred_element_type=jnp.float32).reshape(row_count, blocks, length)
    tail_terms = jnp.dot(next_tail, lower_half, preferred_element_type=jnp.float32).reshape(row_count, 1, length)
    result = own_terms + jnp.concatenate([next_terms[:, 1:], tail_terms], axis=1)
    return result.reshape(row_count, cell_count).astype(jnp.bfloat16)


def doppler_table(pulses):
    index_all = jnp.arange(pulses, dtype=jnp.int32)
    phase_angle = ((index_all[:, None] * index_all[None, :]) % pulses).astype(jnp.float32) * (2.0 * math.pi / pulses)
    window_taper = 0.5 - 0.5 * jnp.cos((index_all.astype(jnp.float32) + 0.5) * (2.0 * math.pi / pulses))
    cosine = window_taper[None, :] * jnp.cos(phase_angle)
    sine_part = window_taper[None, :] * jnp.sin(phase_angle)
    top_rows = jnp.concatenate([cosine, sine_part], axis=1)
    bottom_rows = jnp.concatenate([-sine_part, cosine], axis=1)
    return jnp.concatenate([top_rows, bottom_rows], axis=0).astype(jnp.bfloat16)


def power_of(table, compressed):
    pulses = compressed.shape[1]
    stacked = compressed.reshape(2 * pulses, compressed.shape[2])
    spectrum = jnp.dot(table, stacked, preferred_element_type=jnp.float32)
    return spectrum[:pulses] * spectrum[:pulses] + spectrum[pulses:] * spectrum[pulses:]


def range_sums(padded, half_width, margin):
    cell_count = padded.shape[-1] - 2 * margin
    running = padded[..., margin - half_width:margin - half_width + cell_count]
    for offset in range(margin - half_width + 1, margin + half_width + 1):
        running = running + padded[..., offset:offset + cell_count]
    return running


def slice_sums(wrapped, half_width, reach, pulses):
    running = wrapped[reach - half_width:reach - half_width + pulses]
    for offset in range(reach - half_width + 1, reach + half_width + 1):
        running = running + wrapped[offset:offset + pulses]
    return running


def cfar_ratio(padded, valid_mask):
    margin = WIN_R // 2
    reach = WIN_D // 2
    pulses = padded.shape[0]
    wrapped = jnp.concatenate([padded[pulses - reach:], padded, padded[:reach]], axis=0)
    wide_sums = range_sums(wrapped, WIN_R // 2, margin)
    guard_sums = range_sums(wrapped, GUARD_R // 2, margin)
    train_sums = slice_sums(wide_sums, WIN_D // 2, reach, pulses) - slice_sums(guard_sums, GUARD_D // 2, reach, pulses)
    train_count = range_sums(valid_mask, WIN_R // 2, margin) * WIN_D - range_sums(valid_mask, GUARD_R // 2, margin) * GUARD_D
    noise_level = train_sums / train_count[None, :]
    center_power = padded[:, margin:padded.shape[1] - margin]
    return center_power / noise_level


def reference(echoes, phase_code):
    pulses = echoes.shape[1]
    cell_count = echoes.shape[2]
    length = phase_code.shape[0]
    echo_rows = echoes.reshape(2 * pulses, cell_count)
    next_tail = jnp.zeros((2 * pulses, length), jnp.bfloat16)
    compressed = compress_rows(echo_rows, next_tail, toeplitz_pair(phase_code)).reshape(2, pulses, cell_count)
    power_map = power_of(doppler_table(pulses), compressed)
    margin = WIN_R // 2
    padded = jnp.pad(power_map, ((0, 0), (margin, margin)))
    valid_mask = jnp.pad(jnp.ones((cell_count,), jnp.float32), (margin, margin))
    return cfar_ratio(padded, valid_mask)
```

```python
import functools
import math

import jax
import jax.numpy as jnp
import numpy as np
from jax import lax
from jax.experimental import pallas as pl
from jax.experimental.pallas import tpu as pltpu
from jax.sharding import PartitionSpec as P

WIN_R = 33
WIN_D = 9
GUARD_R = 5
GUARD_D = 3
LANES = 128
HALO = WIN_R // 2
PACK = LANES // HALO
ROW_PAD = 8
DOPPLER_TILE = 256
CFAR_ROWS = 32
MESH = pl.DeviceIdType.MESH


def doppler_table(pulses, local_pulses):
    index_all = np.arange(pulses, dtype=np.int64)
    step = np.float32(2.0 * math.pi / pulses)
    angle = (index_all[:, None] * index_all[None, :] % pulses).astype(np.float32) * step
    taper = np.float32(0.5) - np.float32(0.5) * np.cos((index_all.astype(np.float32) + np.float32(0.5)) * step)
    cosine = taper[None, :] * np.cos(angle)
    sine = taper[None, :] * np.sin(angle)
    table = np.block([[cosine, sine], [-sine, cosine]]).astype(jnp.bfloat16)
    table = table.reshape(2 * pulses, 2, pulses // local_pulses, local_pulses)
    table = table.transpose(0, 2, 1, 3).reshape(2, pulses // DOPPLER_TILE, DOPPLER_TILE, 2 * pulses)
    return table.transpose(1, 0, 2, 3).reshape(2 * pulses, 2 * pulses)


def shifted(x, count, axis):
    size = x.shape[axis]
    return pltpu.roll(x, (-count) % size, axis)


def body(
    n, echoes_hbm, code_ref, table_hbm, out_ref,
    echoes, table, filters, sending, held, power, edge_out, edge_in,
    echo_sem, table_sem, send_sem, recv_sem, edge_send_sem, edge_recv_sem,
):
    me = lax.axis_index("rng")
    taps = code_ref.shape[1]
    rows, all_cells = echoes_hbm.shape
    cells = all_cells // n
    blocks = cells // taps
    bins = table.shape[0] // 2

    echo_copy = pltpu.make_async_copy(echoes_hbm, echoes.at[:, pl.ds(0, all_cells)], echo_sem)
    echo_copy.start()
    table_copy = pltpu.make_async_copy(table_hbm, table, table_sem)
    table_copy.start()

    barrier = pltpu.get_barrier_semaphore()

    @pl.loop(1, n)
    def _(k):
        pl.semaphore_signal(barrier, inc=1, device_id={"rng": lax.rem(me + k, n)}, device_id_type=MESH)

    row = lax.broadcasted_iota(jnp.int32, (taps, taps), 0)
    col = lax.broadcasted_iota(jnp.int32, (taps, taps), 1)
    rolled = jnp.broadcast_to(code_ref[...].astype(jnp.float32), (taps, taps))
    for bit in range((taps - 1).bit_length()):
        rolled = jnp.where((row & (1 << bit)) != 0, pltpu.roll(rolled, 1 << bit, 1), rolled)
    circulant = rolled.T
    filters[pl.ds(0, taps), :] = jnp.where(row >= col, circulant, 0.0).astype(jnp.bfloat16)
    filters[pl.ds(taps, taps), :] = jnp.where(row < col, circulant, 0.0).astype(jnp.bfloat16)
    echoes[:, pl.ds(all_cells, taps)] = jnp.zeros((rows, taps), jnp.bfloat16)

    echo_copy.wait()
    pl.semaphore_wait(barrier, n - 1)

    def compressed(owner):
        parts = [
            echoes[:, pl.ds(pl.multiple_of(owner * cells + b * taps, taps), taps)] for b in range(blocks + 1)
        ]
        pairs = jnp.concatenate(
            [jnp.concatenate(parts[:-1], axis=0), jnp.concatenate(parts[1:], axis=0)], axis=1
        )
        made = jnp.dot(pairs, filters[...], preferred_element_type=jnp.float32).astype(jnp.bfloat16)
        return [made[b * rows : (b + 1) * rows] for b in range(blocks)]

    def block_copy(slot, owner):
        return pltpu.make_async_remote_copy(
            src_ref=sending.at[owner],
            dst_ref=held.at[slot],
            send_sem=send_sem.at[owner],
            recv_sem=recv_sem.at[slot],
            device_id={"rng": owner},
            device_id_type=MESH,
        )

    @pl.loop(1, n)
    def _(k):
        owner = lax.rem(me + k, n)
        for b, part in enumerate(compressed(owner)):
            sending[owner, :, b * taps : (b + 1) * taps] = part
        block_copy(me, owner).start()

    for b, part in enumerate(compressed(me)):
        held[me, :, b * taps : (b + 1) * taps] = part

    table_copy.wait()

    @pl.loop(1, n)
    def _(k):
        block_copy(lax.rem(me + n - k, n), lax.rem(me + k, n)).wait()

    signal = held[...].reshape(n * rows, cells)

    @pl.loop(0, bins // DOPPLER_TILE)
    def _(i):
        made = jnp.dot(
            table[pl.ds(pl.multiple_of(i * 2 * DOPPLER_TILE, 2 * DOPPLER_TILE), 2 * DOPPLER_TILE), :],
            signal,
            preferred_element_type=jnp.float32,
        )
        real, imag = made[:DOPPLER_TILE], made[DOPPLER_TILE:]
        start = pl.multiple_of(i * DOPPLER_TILE + ROW_PAD, ROW_PAD)
        power[pl.ds(start, DOPPLER_TILE), pl.ds(0, cells)] = real * real + imag * imag

    group = bins // PACK
    lane = lax.broadcasted_iota(jnp.int32, (group, LANES), 1)

    def packed(first, turn):
        total = jnp.zeros((group, LANES), jnp.float32)
        for g in range(PACK):
            tile = power[pl.ds(ROW_PAD + g * group, group), pl.ds(first, LANES)]
            total = jnp.where(lane // HALO == g, pltpu.roll(tile, (g * HALO + turn) % LANES, 1), total)
        return total

    edge_out[0] = packed(0, 0)
    edge_out[1] = packed(cells - LANES, HALO)

    def edge_copy(side):
        return pltpu.make_async_remote_copy(
            src_ref=edge_out.at[side],
            dst_ref=edge_in.at[side],
            send_sem=edge_send_sem.at[side],
            recv_sem=edge_recv_sem.at[side],
            device_id={"rng": lax.rem(me + (n - 1 if side == 0 else 1), n)},
            device_id_type=MESH,
        )

    has_left, has_right = me > 0, me < n - 1

    @pl.when(has_left)
    def _():
        edge_copy(0).start()

    @pl.when(has_right)
    def _():
        edge_copy(1).start()

    @pl.when(has_right)
    def _():
        edge_copy(0).wait_recv()

    @pl.when(jnp.logical_not(has_right))
    def _():
        edge_in[0] = jnp.zeros((group, LANES), jnp.float32)

    @pl.when(has_left)
    def _():
        edge_copy(1).wait_recv()

    @pl.when(jnp.logical_not(has_left))
    def _():
        edge_in[1] = jnp.zeros((group, LANES), jnp.float32)

    after, before = edge_in[0], edge_in[1]
    for g in range(PACK):
        tile = jnp.where(
            lane < HALO,
            pltpu.roll(after, (-g * HALO) % LANES, 1),
            jnp.where(lane >= LANES - HALO, pltpu.roll(before, (-g * HALO - HALO) % LANES, 1), 0.0),
        )
        power[pl.ds(ROW_PAD + g * group, group), pl.ds(cells, LANES)] = tile
    power[pl.ds(0, ROW_PAD), :] = power[pl.ds(bins, ROW_PAD), :]
    power[pl.ds(bins + ROW_PAD, ROW_PAD), :] = power[pl.ds(ROW_PAD, ROW_PAD), :]

    position = me * cells + lax.broadcasted_iota(jnp.int32, (1, cells), 1)

    def inside(half):
        return jnp.minimum(position + half, all_cells - 1) - jnp.maximum(position - half, 0) + 1

    count = inside(WIN_R // 2) * WIN_D - inside(GUARD_R // 2) * GUARD_D
    inverse_count = 1.0 / count.astype(jnp.float32)

    @pl.loop(0, bins // CFAR_ROWS)
    def _(i):
        start = pl.multiple_of(i * CFAR_ROWS, CFAR_ROWS)
        x = power[pl.ds(start, CFAR_ROWS + 2 * ROW_PAD), :]
        two = x + shifted(x, 1, 1)
        four = two + shifted(two, 2, 1)
        eight = four + shifted(four, 4, 1)
        sixteen = eight + shifted(eight, 8, 1)
        wide = sixteen + shifted(sixteen, 16, 1) + shifted(x, 32, 1)
        wide = shifted(wide, -(WIN_R // 2), 1)[:, :cells]
        guard = (shifted(four, -2, 1) + shifted(x, 2, 1))[:, :cells]
        pair = wide + shifted(wide, 1, 0)
        quad = pair + shifted(pair, 2, 0)
        nine = quad + shifted(quad, 4, 0) + shifted(wide, 8, 0)
        three = guard + shifted(guard, 1, 0) + shifted(guard, 2, 0)
        train = shifted(nine, ROW_PAD - WIN_D // 2, 0) - shifted(three, ROW_PAD - GUARD_D // 2, 0)
        noise = train[:CFAR_ROWS] * inverse_count
        out_ref[pl.ds(start, CFAR_ROWS), :] = x[ROW_PAD : ROW_PAD + CFAR_ROWS, :cells] / noise

    @pl.when(has_left)
    def _():
        edge_copy(0).wait_send()

    @pl.when(has_right)
    def _():
        edge_copy(1).wait_send()


def solution(mesh):
    n = mesh.shape["rng"]

    def local(echoes, phase_code):
        _, local_pulses, all_cells = echoes.shape
        rows, pulses, cells = 2 * local_pulses, n * local_pulses, all_cells // n
        taps = phase_code.shape[0]
        group = pulses // PACK
        table = jnp.asarray(doppler_table(pulses, local_pulses))
        vmem = pl.BlockSpec(memory_space=pltpu.VMEM)
        hbm = pl.BlockSpec(memory_space=pl.ANY)
        return pl.pallas_call(
            functools.partial(body, n),
            out_shape=jax.ShapeDtypeStruct((pulses, cells), jnp.float32),
            in_specs=[hbm, vmem, hbm],
            out_specs=vmem,
            scratch_shapes=[
                pltpu.VMEM((rows, all_cells + taps), jnp.bfloat16),
                pltpu.VMEM((2 * pulses, 2 * pulses), jnp.bfloat16),
                pltpu.VMEM((2 * taps, taps), jnp.bfloat16),
                pltpu.VMEM((n, rows, cells), jnp.bfloat16),
                pltpu.VMEM((n, rows, cells), jnp.bfloat16),
                pltpu.VMEM((pulses + 2 * ROW_PAD, cells + LANES), jnp.float32),
                pltpu.VMEM((2, group, LANES), jnp.float32),
                pltpu.VMEM((2, group, LANES), jnp.float32),
                pltpu.SemaphoreType.DMA,
                pltpu.SemaphoreType.DMA,
                pltpu.SemaphoreType.DMA((n,)),
                pltpu.SemaphoreType.DMA((n,)),
                pltpu.SemaphoreType.DMA((2,)),
                pltpu.SemaphoreType.DMA((2,)),
            ],
            compiler_params=pltpu.CompilerParams(
                collective_id=0, has_side_effects=True, vmem_limit_bytes=48 << 20
            ),
        )(echoes.reshape(rows, all_cells), phase_code.reshape(1, taps), table)

    return jax.shard_map(
        local, mesh=mesh, in_specs=(P("beam", "rng", None), P()), out_specs=P("beam", "rng"), check_vma=False
    )
```

```python
import functools
import math

import jax
import jax.numpy as jnp
import numpy as np
from jax import lax
from jax.experimental import pallas as pl
from jax.experimental.pallas import tpu as pltpu
from jax.sharding import PartitionSpec as P

WIN_R = 33
WIN_D = 9
GUARD_R = 5
GUARD_D = 3
LANES = 128
HALO = WIN_R // 2
PACK = LANES // HALO
ROW_PAD = 16
CFAR_ROWS = 128
MESH = pl.DeviceIdType.MESH


def doppler_rows(pulses, local_pulses):
    step = np.float32(2.0 * math.pi / pulses)
    index_all = np.arange(pulses, dtype=np.int64)
    bins = np.arange(pulses // 4, dtype=np.int64)
    angle = (bins[:, None] * index_all[None, :] % pulses).astype(np.float32) * step
    taper = np.float32(0.5) - np.float32(0.5) * np.cos((index_all.astype(np.float32) + np.float32(0.5)) * step)
    cosine = taper[None, :] * np.cos(angle)
    sine = taper[None, :] * np.sin(angle)
    table = np.block([[cosine, sine], [-sine, cosine]]).astype(jnp.bfloat16)
    table = table.reshape(pulses // 2, 2, pulses // local_pulses, local_pulses)
    return table.transpose(0, 2, 1, 3).reshape(pulses // 2, 2 * pulses)


def shifted(x, count, axis):
    size = x.shape[axis]
    return pltpu.roll(x, (-count) % size, axis)


def body(
    n, echoes_hbm, code_hbm, rows_hbm, out_ref,
    echoes, code, first_rows, table, filters, bands, outer_out, inner_out, outer_in, inner_in,
    power, high, low, edge_out, edge_in,
    echo_sem, code_sem, table_sem, outer_send, outer_recv, inner_send, inner_recv, edge_send_sem, edge_recv_sem,
):
    me = lax.axis_index("rng")
    taps = code.shape[1]
    rows, all_cells = echoes_hbm.shape
    cells = all_cells // n
    blocks = cells // taps
    bins = table.shape[0] // 2
    tile = bins // 4
    half = LANES

    echo_copy = pltpu.make_async_copy(echoes_hbm, echoes.at[:, pl.ds(0, all_cells)], echo_sem)
    echo_copy.start()
    code_copy = pltpu.make_async_copy(code_hbm, code, code_sem)
    code_copy.start()
    table_copy = pltpu.make_async_copy(rows_hbm, first_rows, table_sem)
    table_copy.start()

    barrier = pltpu.get_barrier_semaphore()

    @pl.loop(1, n)
    def _(k):
        pl.semaphore_signal(barrier, inc=1, device_id={"rng": lax.rem(me + k, n)}, device_id_type=MESH)

    code_copy.wait()
    row = lax.broadcasted_iota(jnp.int32, (taps, taps), 0)
    col = lax.broadcasted_iota(jnp.int32, (taps, taps), 1)
    rolled = jnp.broadcast_to(code[...].astype(jnp.float32), (taps, taps))
    for bit in range((taps - 1).bit_length()):
        rolled = jnp.where((row & (1 << bit)) != 0, pltpu.roll(rolled, 1 << bit, 1), rolled)
    circulant = rolled.T
    filters[pl.ds(0, taps), :] = jnp.where(row >= col, circulant, 0.0).astype(jnp.bfloat16)
    filters[pl.ds(taps, taps), :] = jnp.where(row < col, circulant, 0.0).astype(jnp.bfloat16)
    echoes[:, pl.ds(all_cells, taps)] = jnp.zeros((rows, taps), jnp.bfloat16)

    echo_copy.wait()
    pl.semaphore_wait(barrier, n - 1)

    def compressed(owner):
        parts = [
            echoes[:, pl.ds(pl.multiple_of(owner * cells + b * taps, taps), taps)] for b in range(blocks + 1)
        ]
        pairs = jnp.concatenate(
            [jnp.concatenate(parts[:-1], axis=0), jnp.concatenate(parts[1:], axis=0)], axis=1
        )
        made = jnp.dot(pairs, filters[...], preferred_element_type=jnp.float32).astype(jnp.bfloat16)
        return [made[b * rows : (b + 1) * rows] for b in range(blocks)]

    def outer_copy(slot, owner):
        return pltpu.make_async_remote_copy(
            src_ref=outer_out.at[owner],
            dst_ref=outer_in.at[slot],
            send_sem=outer_send.at[owner],
            recv_sem=outer_recv.at[slot],
            device_id={"rng": owner},
            device_id_type=MESH,
        )

    def inner_copy(slot, owner):
        return pltpu.make_async_remote_copy(
            src_ref=inner_out.at[owner],
            dst_ref=inner_in.at[slot],
            send_sem=inner_send.at[owner],
            recv_sem=inner_recv.at[slot],
            device_id={"rng": owner},
            device_id_type=MESH,
        )

    def place(outer, inner, slot, parts):
        left, right = parts
        outer[slot, :, :half] = left[:, :half]
        outer[slot, :, half:] = right[:, half:]
        inner[slot, :, :half] = left[:, half:]
        inner[slot, :, half:] = right[:, :half]

    @pl.loop(1, n)
    def _(k):
        owner = lax.rem(me + k, n)
        place(outer_out, inner_out, owner, compressed(owner))
        outer_copy(me, owner).start()

    @pl.loop(1, n)
    def _(k):
        inner_copy(me, lax.rem(me + k, n)).start()

    place(outer_in, inner_in, me, compressed(me))

    table_copy.wait()
    column = lax.broadcasted_iota(jnp.int32, (1, 2 * bins), 1)
    for quarter in range(4):
        turn = (column * quarter) % 4
        same = jnp.where(turn == 0, 1.0, jnp.where(turn == 2, -1.0, 0.0)).astype(jnp.bfloat16)
        other = jnp.where(turn == 1, 1.0, jnp.where(turn == 3, -1.0, 0.0)).astype(jnp.bfloat16)

        @pl.loop(0, tile // 32)
        def _(j):
            start = pl.multiple_of(j * 32, 32)
            real = first_rows[pl.ds(start, 32), :]
            imag = first_rows[pl.ds(pl.multiple_of(start + tile, 32), 32), :]
            base = quarter * 2 * tile
            table[pl.ds(pl.multiple_of(base + start, 32), 32), :] = real * same + imag * other
            table[pl.ds(pl.multiple_of(base + tile + start, 32), 32), :] = imag * same - real * other

    distance = (
        lax.broadcasted_iota(jnp.int32, (4 * half, 2 * half), 0)
        - half
        - lax.broadcasted_iota(jnp.int32, (4 * half, 2 * half), 1)
    )
    for side, width in ((0, WIN_R), (1, GUARD_R)):
        band = jnp.where(jnp.abs(distance) <= width // 2, 1.0, 0.0).astype(jnp.bfloat16)
        for part in range(2):
            bands[part * 4 * half : (part + 1) * 4 * half, side * 2 * half : (side + 1) * 2 * half] = band

    def keep(start, count, lane_tile, value):
        power[pl.ds(start, count), lane_tile * LANES : (lane_tile + 1) * LANES] = value
        top = value.astype(jnp.bfloat16)
        rest = (value - top.astype(jnp.float32)).astype(jnp.bfloat16)
        for at in ((lane_tile + 1,) if lane_tile < 4 else (0, 5)):
            high[pl.ds(start, count), at * LANES : (at + 1) * LANES] = top
            low[pl.ds(start, count), at * LANES : (at + 1) * LANES] = rest

    def transform(held, lane_tiles):
        signal = held[...].reshape(n * rows, 2 * half)

        @pl.loop(0, 4)
        def _(i):
            made = jnp.dot(
                table[pl.ds(pl.multiple_of(i * 2 * tile, 2 * tile), 2 * tile), :],
                signal,
                preferred_element_type=jnp.float32,
            )
            real, imag = made[:tile], made[tile:]
            value = real * real + imag * imag
            start = pl.multiple_of(i * tile + ROW_PAD, ROW_PAD)
            keep(start, tile, lane_tiles[0], value[:, :half])
            keep(start, tile, lane_tiles[1], value[:, half:])

    @pl.loop(1, n)
    def _(k):
        outer_copy(lax.rem(me + n - k, n), lax.rem(me + k, n)).wait()

    transform(outer_in, (0, 3))

    group = bins // PACK
    lane = lax.broadcasted_iota(jnp.int32, (group, LANES), 1)

    def packed(first, turn):
        total = jnp.zeros((group, LANES), jnp.float32)
        for g in range(PACK):
            held = power[pl.ds(ROW_PAD + g * group, group), pl.ds(first, LANES)]
            total = jnp.where(lane // HALO == g, pltpu.roll(held, (g * HALO + turn) % LANES, 1), total)
        return total

    edge_out[0] = packed(0, 0)
    edge_out[1] = packed(cells - LANES, HALO)

    def edge_copy(side):
        return pltpu.make_async_remote_copy(
            src_ref=edge_out.at[side],
            dst_ref=edge_in.at[side],
            send_sem=edge_send_sem.at[side],
            recv_sem=edge_recv_sem.at[side],
            device_id={"rng": lax.rem(me + (n - 1 if side == 0 else 1), n)},
            device_id_type=MESH,
        )

    has_left, has_right = me > 0, me < n - 1

    @pl.when(has_left)
    def _():
        edge_copy(0).start()

    @pl.when(has_right)
    def _():
        edge_copy(1).start()

    @pl.when(has_right)
    def _():
        edge_copy(0).wait_recv()

    @pl.when(jnp.logical_not(has_right))
    def _():
        edge_in[0] = jnp.zeros((group, LANES), jnp.float32)

    @pl.when(has_left)
    def _():
        edge_copy(1).wait_recv()

    @pl.when(jnp.logical_not(has_left))
    def _():
        edge_in[1] = jnp.zeros((group, LANES), jnp.float32)

    after, before = edge_in[0], edge_in[1]
    for g in range(PACK):
        ends = jnp.where(
            lane < HALO,
            pltpu.roll(after, (-g * HALO) % LANES, 1),
            jnp.where(lane >= LANES - HALO, pltpu.roll(before, (-g * HALO - HALO) % LANES, 1), 0.0),
        )
        keep(ROW_PAD + g * group, group, 4, ends)

    @pl.loop(1, n)
    def _(k):
        inner_copy(lax.rem(me + n - k, n), lax.rem(me + k, n)).wait()

    transform(inner_in, (1, 2))
    for ref in (high, low):
        ref[pl.ds(0, ROW_PAD), :] = ref[pl.ds(bins, ROW_PAD), :]
        ref[pl.ds(bins + ROW_PAD, ROW_PAD), :] = ref[pl.ds(ROW_PAD, ROW_PAD), :]

    position = me * cells + lax.broadcasted_iota(jnp.int32, (1, cells), 1)

    def inside(half):
        return jnp.minimum(position + half, all_cells - 1) - jnp.maximum(position - half, 0) + 1

    count = inside(WIN_R // 2) * WIN_D - inside(GUARD_R // 2) * GUARD_D
    inverse_count = 1.0 / count.astype(jnp.float32)

    @pl.loop(0, bins // CFAR_ROWS)
    def _(i):
        start = pl.multiple_of(i * CFAR_ROWS, CFAR_ROWS)
        span = CFAR_ROWS + 2 * ROW_PAD
        center = power[pl.ds(pl.multiple_of(start + ROW_PAD, ROW_PAD), CFAR_ROWS), :]
        for side in range(2):
            lanes = slice(side * 2 * half, side * 2 * half + 4 * half)
            both = jnp.concatenate([high[pl.ds(start, span), lanes], low[pl.ds(start, span), lanes]], axis=1)
            sums = jnp.dot(both, bands[...], preferred_element_type=jnp.float32)
            wide, guard = sums[:, : 2 * half], sums[:, 2 * half :]
            pair = wide + shifted(wide, 1, 0)
            quad = pair + shifted(pair, 2, 0)
            nine = quad + shifted(quad, 4, 0) + shifted(wide, 8, 0)
            three = guard + shifted(guard, 1, 0) + shifted(guard, 2, 0)
            train = shifted(nine, ROW_PAD - WIN_D // 2, 0) - shifted(three, ROW_PAD - GUARD_D // 2, 0)
            own = slice(side * 2 * half, (side + 1) * 2 * half)
            noise = train[:CFAR_ROWS] * inverse_count[:, own]
            out_ref[pl.ds(start, CFAR_ROWS), own] = center[:, own] / noise

    @pl.when(has_left)
    def _():
        edge_copy(0).wait_send()

    @pl.when(has_right)
    def _():
        edge_copy(1).wait_send()


def solution(mesh):
    n = mesh.shape["rng"]

    def local(echoes, phase_code):
        _, local_pulses, all_cells = echoes.shape
        rows, pulses, cells = 2 * local_pulses, n * local_pulses, all_cells // n
        taps = phase_code.shape[0]
        group = pulses // PACK
        if cells != 2 * taps or cells != 4 * LANES or local_pulses % 4:
            raise ValueError("unsupported shape")
        hbm = pl.BlockSpec(memory_space=pl.ANY)
        return pl.pallas_call(
            functools.partial(body, n),
            out_shape=jax.ShapeDtypeStruct((pulses, cells), jnp.float32),
            in_specs=[hbm, hbm, hbm],
            out_specs=pl.BlockSpec(memory_space=pltpu.VMEM),
            scratch_shapes=[
                pltpu.VMEM((rows, all_cells + taps), jnp.bfloat16),
                pltpu.VMEM((1, taps), jnp.int32),
                pltpu.VMEM((pulses // 2, 2 * pulses), jnp.bfloat16),
                pltpu.VMEM((2 * pulses, 2 * pulses), jnp.bfloat16),
                pltpu.VMEM((2 * taps, taps), jnp.bfloat16),
                pltpu.VMEM((8 * LANES, 4 * LANES), jnp.bfloat16),
                pltpu.VMEM((n, rows, 2 * LANES), jnp.bfloat16),
                pltpu.VMEM((n, rows, 2 * LANES), jnp.bfloat16),
                pltpu.VMEM((n, rows, 2 * LANES), jnp.bfloat16),
                pltpu.VMEM((n, rows, 2 * LANES), jnp.bfloat16),
                pltpu.VMEM((pulses + 2 * ROW_PAD, cells + LANES), jnp.float32),
                pltpu.VMEM((pulses + 2 * ROW_PAD, cells + 2 * LANES), jnp.bfloat16),
                pltpu.VMEM((pulses + 2 * ROW_PAD, cells + 2 * LANES), jnp.bfloat16),
                pltpu.VMEM((2, group, LANES), jnp.float32),
                pltpu.VMEM((2, group, LANES), jnp.float32),
                pltpu.SemaphoreType.DMA,
                pltpu.SemaphoreType.DMA,
                pltpu.SemaphoreType.DMA,
                pltpu.SemaphoreType.DMA((n,)),
                pltpu.SemaphoreType.DMA((n,)),
                pltpu.SemaphoreType.DMA((n,)),
                pltpu.SemaphoreType.DMA((n,)),
                pltpu.SemaphoreType.DMA((2,)),
                pltpu.SemaphoreType.DMA((2,)),
            ],
            compiler_params=pltpu.CompilerParams(
                collective_id=0, has_side_effects=True, vmem_limit_bytes=60 << 20
            ),
        )(echoes.reshape(rows, all_cells), phase_code.reshape(1, taps),
          jnp.asarray(doppler_rows(pulses, local_pulses)))

    return jax.shard_map(
        local, mesh=mesh, in_specs=(P("beam", "rng", None), P()), out_specs=P("beam", "rng"), check_vma=False
    )
```

```python
import functools
import math

import jax
import jax.numpy as jnp
import numpy as np
from jax import lax
from jax.experimental import pallas as pl
from jax.experimental.pallas import tpu as pltpu
from jax.sharding import PartitionSpec as P

WIN_R = 33
WIN_D = 9
GUARD_R = 5
GUARD_D = 3
LANES = 128
HALO = WIN_R // 2
PACK = LANES // HALO
ROW_PAD = 16
CFAR_ROWS = 256
MESH = pl.DeviceIdType.MESH


def doppler_rows(pulses, local_pulses):
    step = np.float32(2.0 * math.pi / pulses)
    index_all = np.arange(pulses, dtype=np.int64)
    bins = np.arange(pulses // 4, dtype=np.int64)
    angle = (bins[:, None] * index_all[None, :] % pulses).astype(np.float32) * step
    taper = np.float32(0.5) - np.float32(0.5) * np.cos((index_all.astype(np.float32) + np.float32(0.5)) * step)
    cosine = taper[None, :] * np.cos(angle)
    sine = taper[None, :] * np.sin(angle)
    table = np.block([[cosine, sine], [-sine, cosine]]).astype(jnp.bfloat16)
    table = table.reshape(pulses // 2, 2, pulses // local_pulses, local_pulses)
    return table.transpose(0, 2, 1, 3).reshape(pulses // 2, 2 * pulses)


def shifted(x, count, axis):
    size = x.shape[axis]
    return pltpu.roll(x, (-count) % size, axis)


def body(
    n, echoes_hbm, code_hbm, rows_hbm, out_hbm,
    echoes, code, first_rows, table, filters, bands, outer_out, inner_out, outer_in, inner_in,
    power, high, low, result, edge_out, edge_in,
    echo_sem, code_sem, table_sem, outer_send, outer_recv, inner_send, inner_recv, edge_send_sem, edge_recv_sem, result_sem,
):
    me = lax.axis_index("rng")
    taps = code.shape[1]
    rows, all_cells = echoes_hbm.shape
    cells = all_cells // n
    blocks = cells // taps
    bins = table.shape[0] // 2
    tile = bins // 4
    half = LANES

    echo_copy = pltpu.make_async_copy(echoes_hbm, echoes.at[:, pl.ds(0, all_cells)], echo_sem)
    echo_copy.start()
    code_copy = pltpu.make_async_copy(code_hbm, code, code_sem)
    code_copy.start()
    table_copy = pltpu.make_async_copy(rows_hbm, first_rows, table_sem)
    table_copy.start()

    barrier = pltpu.get_barrier_semaphore()

    @pl.loop(1, n)
    def _(k):
        pl.semaphore_signal(barrier, inc=1, device_id={"rng": lax.rem(me + k, n)}, device_id_type=MESH)

    code_copy.wait()
    row = lax.broadcasted_iota(jnp.int32, (taps, taps), 0)
    col = lax.broadcasted_iota(jnp.int32, (taps, taps), 1)
    rolled = jnp.broadcast_to(code[...].astype(jnp.float32), (taps, taps))
    for bit in range((taps - 1).bit_length()):
        rolled = jnp.where((row & (1 << bit)) != 0, pltpu.roll(rolled, 1 << bit, 1), rolled)
    circulant = rolled.T
    filters[pl.ds(0, taps), :] = jnp.where(row >= col, circulant, 0.0).astype(jnp.bfloat16)
    filters[pl.ds(taps, taps), :] = jnp.where(row < col, circulant, 0.0).astype(jnp.bfloat16)
    echoes[:, pl.ds(all_cells, taps)] = jnp.zeros((rows, taps), jnp.bfloat16)

    echo_copy.wait()
    pl.semaphore_wait(barrier, n - 1)

    def compressed(owner):
        parts = [
            echoes[:, pl.ds(pl.multiple_of(owner * cells + b * taps, taps), taps)] for b in range(blocks + 1)
        ]
        pairs = jnp.concatenate(
            [jnp.concatenate(parts[:-1], axis=0), jnp.concatenate(parts[1:], axis=0)], axis=1
        )
        made = jnp.dot(pairs, filters[...], preferred_element_type=jnp.float32).astype(jnp.bfloat16)
        return [made[b * rows : (b + 1) * rows] for b in range(blocks)]

    def outer_copy(slot, owner):
        return pltpu.make_async_remote_copy(
            src_ref=outer_out.at[owner],
            dst_ref=outer_in.at[slot],
            send_sem=outer_send.at[owner],
            recv_sem=outer_recv.at[slot],
            device_id={"rng": owner},
            device_id_type=MESH,
        )

    def inner_copy(slot, owner):
        return pltpu.make_async_remote_copy(
            src_ref=inner_out.at[owner],
            dst_ref=inner_in.at[slot],
            send_sem=inner_send.at[owner],
            recv_sem=inner_recv.at[slot],
            device_id={"rng": owner},
            device_id_type=MESH,
        )

    def place(outer, inner, slot, parts):
        left, right = parts
        outer[slot, :, :half] = left[:, :half]
        outer[slot, :, half:] = right[:, half:]
        inner[slot, :, :half] = left[:, half:]
        inner[slot, :, half:] = right[:, :half]

    @pl.loop(1, n)
    def _(k):
        owner = lax.rem(me + k, n)
        place(outer_out, inner_out, owner, compressed(owner))
        outer_copy(me, owner).start()

    @pl.loop(1, n)
    def _(k):
        inner_copy(me, lax.rem(me + k, n)).start()

    place(outer_in, inner_in, me, compressed(me))

    table_copy.wait()
    column = lax.broadcasted_iota(jnp.int32, (1, 2 * bins), 1)
    for quarter in range(4):
        turn = (column * quarter) % 4
        same = jnp.where(turn == 0, 1.0, jnp.where(turn == 2, -1.0, 0.0)).astype(jnp.bfloat16)
        other = jnp.where(turn == 1, 1.0, jnp.where(turn == 3, -1.0, 0.0)).astype(jnp.bfloat16)

        @pl.loop(0, tile // 32)
        def _(j):
            start = pl.multiple_of(j * 32, 32)
            real = first_rows[pl.ds(start, 32), :]
            imag = first_rows[pl.ds(pl.multiple_of(start + tile, 32), 32), :]
            base = quarter * 2 * tile
            table[pl.ds(pl.multiple_of(base + start, 32), 32), :] = real * same + imag * other
            table[pl.ds(pl.multiple_of(base + tile + start, 32), 32), :] = imag * same - real * other

    distance = (
        lax.broadcasted_iota(jnp.int32, (4 * half, 2 * half), 0)
        - half
        - lax.broadcasted_iota(jnp.int32, (4 * half, 2 * half), 1)
    )
    for side, width in ((0, WIN_R), (1, GUARD_R)):
        band = jnp.where(jnp.abs(distance) <= width // 2, 1.0, 0.0).astype(jnp.bfloat16)
        for part in range(2):
            bands[part * 4 * half : (part + 1) * 4 * half, side * 2 * half : (side + 1) * 2 * half] = band

    def keep(start, count, lane_tile, value):
        power[pl.ds(start, count), lane_tile * LANES : (lane_tile + 1) * LANES] = value
        top = value.astype(jnp.bfloat16)
        rest = (value - top.astype(jnp.float32)).astype(jnp.bfloat16)
        for at in ((lane_tile + 1,) if lane_tile < 4 else (0, 5)):
            high[pl.ds(start, count), at * LANES : (at + 1) * LANES] = top
            low[pl.ds(start, count), at * LANES : (at + 1) * LANES] = rest

    def transform(held, lane_tiles):
        signal = held[...].reshape(n * rows, 2 * half)

        together = 2

        @pl.loop(0, 4 // together)
        def _(i):
            size = 2 * together * tile
            made = jnp.dot(
                table[pl.ds(pl.multiple_of(i * size, size), size), :], signal, preferred_element_type=jnp.float32
            )
            for t in range(together):
                real = made[2 * t * tile : (2 * t + 1) * tile]
                imag = made[(2 * t + 1) * tile : (2 * t + 2) * tile]
                value = real * real + imag * imag
                start = pl.multiple_of((i * together + t) * tile + ROW_PAD, ROW_PAD)
                keep(start, tile, lane_tiles[0], value[:, :half])
                keep(start, tile, lane_tiles[1], value[:, half:])

    @pl.loop(1, n)
    def _(k):
        outer_copy(lax.rem(me + n - k, n), lax.rem(me + k, n)).wait()

    transform(outer_in, (0, 3))

    group = bins // PACK
    lane = lax.broadcasted_iota(jnp.int32, (group, LANES), 1)

    def packed(first, turn):
        total = jnp.zeros((group, LANES), jnp.float32)
        for g in range(PACK):
            held = power[pl.ds(ROW_PAD + g * group, group), pl.ds(first, LANES)]
            total = jnp.where(lane // HALO == g, pltpu.roll(held, (g * HALO + turn) % LANES, 1), total)
        return total

    edge_out[0] = packed(0, 0)
    edge_out[1] = packed(cells - LANES, HALO)

    def edge_copy(side):
        return pltpu.make_async_remote_copy(
            src_ref=edge_out.at[side],
            dst_ref=edge_in.at[side],
            send_sem=edge_send_sem.at[side],
            recv_sem=edge_recv_sem.at[side],
            device_id={"rng": lax.rem(me + (n - 1 if side == 0 else 1), n)},
            device_id_type=MESH,
        )

    has_left, has_right = me > 0, me < n - 1

    @pl.when(has_left)
    def _():
        edge_copy(0).start()

    @pl.when(has_right)
    def _():
        edge_copy(1).start()

    @pl.when(has_right)
    def _():
        edge_copy(0).wait_recv()

    @pl.when(jnp.logical_not(has_right))
    def _():
        edge_in[0] = jnp.zeros((group, LANES), jnp.float32)

    @pl.when(has_left)
    def _():
        edge_copy(1).wait_recv()

    @pl.when(jnp.logical_not(has_left))
    def _():
        edge_in[1] = jnp.zeros((group, LANES), jnp.float32)

    after, before = edge_in[0], edge_in[1]
    for g in range(PACK):
        ends = jnp.where(
            lane < HALO,
            pltpu.roll(after, (-g * HALO) % LANES, 1),
            jnp.where(lane >= LANES - HALO, pltpu.roll(before, (-g * HALO - HALO) % LANES, 1), 0.0),
        )
        keep(ROW_PAD + g * group, group, 4, ends)

    @pl.loop(1, n)
    def _(k):
        inner_copy(lax.rem(me + n - k, n), lax.rem(me + k, n)).wait()

    transform(inner_in, (1, 2))
    for ref in (high, low):
        ref[pl.ds(0, ROW_PAD), :] = ref[pl.ds(bins, ROW_PAD), :]
        ref[pl.ds(bins + ROW_PAD, ROW_PAD), :] = ref[pl.ds(ROW_PAD, ROW_PAD), :]

    position = me * cells + lax.broadcasted_iota(jnp.int32, (1, cells), 1)

    def inside(half):
        return jnp.minimum(position + half, all_cells - 1) - jnp.maximum(position - half, 0) + 1

    count = inside(WIN_R // 2) * WIN_D - inside(GUARD_R // 2) * GUARD_D
    inverse_count = 1.0 / count.astype(jnp.float32)

    def result_copy(i):
        own = pl.ds(pl.multiple_of(i * CFAR_ROWS, CFAR_ROWS), CFAR_ROWS)
        return pltpu.make_async_copy(result.at[own, :], out_hbm.at[own, :], result_sem.at[i])

    @pl.loop(0, bins // CFAR_ROWS)
    def _(i):
        start = pl.multiple_of(i * CFAR_ROWS, CFAR_ROWS)
        span = CFAR_ROWS + 2 * ROW_PAD
        center = power[pl.ds(pl.multiple_of(start + ROW_PAD, ROW_PAD), CFAR_ROWS), :]
        for side in range(2):
            lanes = slice(side * 2 * half, side * 2 * half + 4 * half)
            both = jnp.concatenate([high[pl.ds(start, span), lanes], low[pl.ds(start, span), lanes]], axis=1)
            sums = jnp.dot(both, bands[...], preferred_element_type=jnp.float32)
            wide, guard = sums[:, : 2 * half], sums[:, 2 * half :]
            pair = wide + shifted(wide, 1, 0)
            quad = pair + shifted(pair, 2, 0)
            nine = quad + shifted(quad, 4, 0) + shifted(wide, 8, 0)
            three = guard + shifted(guard, 1, 0) + shifted(guard, 2, 0)
            train = shifted(nine, ROW_PAD - WIN_D // 2, 0) - shifted(three, ROW_PAD - GUARD_D // 2, 0)
            own = slice(side * 2 * half, (side + 1) * 2 * half)
            noise = train[:CFAR_ROWS] * inverse_count[:, own]
            result[pl.ds(start, CFAR_ROWS), own] = center[:, own] / noise
        result_copy(i).start()

    @pl.when(has_left)
    def _():
        edge_copy(0).wait_send()

    @pl.when(has_right)
    def _():
        edge_copy(1).wait_send()

    @pl.loop(0, bins // CFAR_ROWS)
    def _(i):
        result_copy(i).wait()


def solution(mesh):
    n = mesh.shape["rng"]

    def local(echoes, phase_code):
        _, local_pulses, all_cells = echoes.shape
        rows, pulses, cells = 2 * local_pulses, n * local_pulses, all_cells // n
        taps = phase_code.shape[0]
        group = pulses // PACK
        if cells != 2 * taps or cells != 4 * LANES or local_pulses % 4:
            raise ValueError("unsupported shape")
        hbm = pl.BlockSpec(memory_space=pl.ANY)
        return pl.pallas_call(
            functools.partial(body, n),
            out_shape=jax.ShapeDtypeStruct((pulses, cells), jnp.float32),
            in_specs=[hbm, hbm, hbm],
            out_specs=hbm,
            scratch_shapes=[
                pltpu.VMEM((rows, all_cells + taps), jnp.bfloat16),
                pltpu.VMEM((1, taps), jnp.int32),
                pltpu.VMEM((pulses // 2, 2 * pulses), jnp.bfloat16),
                pltpu.VMEM((2 * pulses, 2 * pulses), jnp.bfloat16),
                pltpu.VMEM((2 * taps, taps), jnp.bfloat16),
                pltpu.VMEM((8 * LANES, 4 * LANES), jnp.bfloat16),
                pltpu.VMEM((n, rows, 2 * LANES), jnp.bfloat16),
                pltpu.VMEM((n, rows, 2 * LANES), jnp.bfloat16),
                pltpu.VMEM((n, rows, 2 * LANES), jnp.bfloat16),
                pltpu.VMEM((n, rows, 2 * LANES), jnp.bfloat16),
                pltpu.VMEM((pulses + 2 * ROW_PAD, cells + LANES), jnp.float32),
                pltpu.VMEM((pulses + 2 * ROW_PAD, cells + 2 * LANES), jnp.bfloat16),
                pltpu.VMEM((pulses + 2 * ROW_PAD, cells + 2 * LANES), jnp.bfloat16),
                pltpu.VMEM((pulses, cells), jnp.float32),
                pltpu.VMEM((2, group, LANES), jnp.float32),
                pltpu.VMEM((2, group, LANES), jnp.float32),
                pltpu.SemaphoreType.DMA,
                pltpu.SemaphoreType.DMA,
                pltpu.SemaphoreType.DMA,
                pltpu.SemaphoreType.DMA((n,)),
                pltpu.SemaphoreType.DMA((n,)),
                pltpu.SemaphoreType.DMA((n,)),
                pltpu.SemaphoreType.DMA((n,)),
                pltpu.SemaphoreType.DMA((2,)),
                pltpu.SemaphoreType.DMA((2,)),
                pltpu.SemaphoreType.DMA((pulses // CFAR_ROWS,)),
            ],
            compiler_params=pltpu.CompilerParams(
                collective_id=0, has_side_effects=True, vmem_limit_bytes=60 << 20
            ),
        )(echoes.reshape(rows, all_cells), phase_code.reshape(1, taps),
          jnp.asarray(doppler_rows(pulses, local_pulses)))

    return jax.shard_map(
        local, mesh=mesh, in_specs=(P("beam", "rng", None), P()), out_specs=P("beam", "rng"), check_vma=False
    )
```
